32 devices in a mesh: gx: 4 (over y, x), gy: 8 (over z, core).
Axes of the slice: x: 2, y: 2, z: 4, core: 2. Of those that a mesh axis runs over, the one named last changes fastest.
Arguments:
- conserved: float32 [5, 4, 4, 4, 16, 16, 128], P(None, None, None, None, 'gx', 'gy'), as said below
- troubled_list: int32 [16384], P(('gx', 'gy')), may hold values from 0 to 1024, as said below
- widths_x: float32 [16], replicated, may hold values from 1 to 3
- widths_y: float32 [16], replicated, may hold values from 1 to 3
- widths_z: float32 [128], replicated, may hold values from 1 to 3
- speed_x: float32 [16], replicated, may hold values from -0.5 to 0.5
- speed_y: float32 [16], replicated, may hold values from -0.5 to 0.5
- speed_z: float32 [128], replicated, may hold values from -0.5 to 0.5
Outputs:
- advanced: float32 [5, 4, 4, 4, 16, 16, 128], P(None, None, None, None, 'gx', 'gy')
- hessian: float32 [6, 16, 16, 128], P(None, 'gx', 'gy')
The draws below stay inside these ranges and needn't reach their ends.
Inputs may be any that keep to these rules, and one draw needn't show every extreme that they name: `conserved`: density lies between 0.5 and 2 and the pressure computed from the state between 0.5 and 2 at every node. `troubled_list`: in each device's block the first c entries are distinct element indices in increasing order and the rest equal 1024; c is at most 512 and reaches 512 on some device, and the c of all devices sum to exactly 8192.
All inputs are finite; a program needn't handle non-finite values.
Results may differ from the reference program's by a relative error of at most 0.0003.
Values sent between devices are 32-bit elements; how exact they have to be, the bound alone decides.
A program may use at most 64 MiB of HBM per device.

```python
import math
import jax
import jax.numpy as jnp
import numpy as np
from jax import lax

EX = 4
EY = 2
EZ = 128
BAL = 256
NEX = 16
NEY = 16
N_GX = 4
N_GY = 8
DEVICES = 32


def draw_conserved(key, part):
    subkeys = jax.random.split(key, 3)
    grid_shape = (4, 4, 4, NEX, NEY, EZ)
    density = jnp.exp(jax.random.uniform(subkeys[0], grid_shape, jnp.float32, math.log(0.5), math.log(2.0)))
    velocity = jnp.clip(0.4 * jax.random.normal(subkeys[1], (3,) + grid_shape, jnp.float32), -1.5, 1.5)
    pressure = jnp.exp(jax.random.uniform(subkeys[2], grid_shape, jnp.float32, math.log(0.5), math.log(2.0)))
    momentum = density[None] * velocity
    energy = pressure / 0.4 + 0.5 * density * (velocity[0] * velocity[0] + velocity[1] * velocity[1] + velocity[2] * velocity[2])
    return jnp.concatenate([density[None], momentum, energy[None]], axis=0).astype(jnp.float32)


def draw_troubled_list(key, part):
    elements = EX * EY * EZ
    key_order, key_spread, key_pick = jax.random.split(key, 3)
    placing = jax.random.permutation(key_order, DEVICES)
    spreads = jax.random.randint(key_spread, (DEVICES // 2,), 0, BAL + 1).at[0].set(BAL)
    positions = jnp.arange(DEVICES)
    signed = jnp.where(positions % 2 == 0, 1, -1) * spreads[positions // 2]
    counts = jnp.zeros((DEVICES,), jnp.int32).at[placing].set((BAL + signed).astype(jnp.int32))

    def pick_one(device_key, count):
        ranking = jax.random.permutation(device_key, elements)
        element_ids = jnp.arange(elements, dtype=jnp.int32)
        scores = jnp.where(ranking < count, element_ids, elements + element_ids)
        ordered = jnp.sort(scores)[:2 * BAL]
        return jnp.where(ordered < elements, ordered, elements)
    lists = jax.vmap(pick_one)(jax.random.split(key_pick, DEVICES), counts)
    return lists.reshape(-1).astype(jnp.int32)


def setup_inputs(seed: int = 0) -> dict:
    seeds = jax.random.split(jax.random.key(seed), 9)
    return {
        "conserved": draw_conserved(jax.random.fold_in(seeds[8], 71), 0),
        "troubled_list": draw_troubled_list(jax.random.fold_in(seeds[8], 71), 0),
        "widths_x": jnp.clip(jnp.exp(jax.random.uniform(seeds[2], (NEX,), jnp.float32, math.log(1.0), math.log(3.0))), 1.0, 3.0),
        "widths_y": jnp.clip(jnp.exp(jax.random.uniform(seeds[3], (NEY,), jnp.float32, math.log(1.0), math.log(3.0))), 1.0, 3.0),
        "widths_z": jnp.clip(jnp.exp(jax.random.uniform(seeds[4], (EZ,), jnp.float32, math.log(1.0), math.log(3.0))), 1.0, 3.0),
        "speed_x": jnp.clip(jax.random.uniform(seeds[5], (NEX,), jnp.float32, -0.5, 0.5), -0.5, 0.5),
        "speed_y": jnp.clip(jax.random.uniform(seeds[6], (NEY,), jnp.float32, -0.5, 0.5), -0.5, 0.5),
        "speed_z": jnp.clip(jax.random.uniform(seeds[7], (EZ,), jnp.float32, -0.5, 0.5), -0.5, 0.5),
    }


time_step = 0.05
gamma_ratio = 1.4

def lgl_tables():
    nodes = np.array([-1.0, -1.0 / np.sqrt(5.0), 1.0 / np.sqrt(5.0), 1.0])
    weights = np.array([1.0 / 6.0, 5.0 / 6.0, 5.0 / 6.0, 1.0 / 6.0])
    barycentric = np.ones(4)
    for row_a in range(4):
        for row_b in range(4):
            if row_a != row_b:
                barycentric[row_a] = barycentric[row_a] / (nodes[row_a] - nodes[row_b])
    deriv = np.zeros((4, 4))
    for row_a in range(4):
        for row_b in range(4):
            if row_a != row_b:
                deriv[row_a, row_b] = barycentric[row_b] / barycentric[row_a] / (nodes[row_a] - nodes[row_b])
    for row_a in range(4):
        deriv[row_a, row_a] = -np.sum(deriv[row_a])
    return (nodes, weights, deriv)

def euler_flux(conserved, direction, mesh_speed):
    density = conserved[0]
    normal_vel = conserved[direction + 1] / density
    kinetic = 0.5 * (conserved[1] * conserved[1] + conserved[2] * conserved[2] + conserved[3] * conserved[3]) / density
    pressure = (gamma_ratio - 1.0) * (conserved[4] - kinetic)
    relative = normal_vel - mesh_speed
    columns_out = [conserved[component] * relative for component in range(5)]
    columns_out[direction + 1] = columns_out[direction + 1] + pressure
    columns_out[4] = columns_out[4] + pressure * normal_vel
    sound = jnp.sqrt(gamma_ratio * pressure / density)
    return (jnp.stack(columns_out), jnp.abs(relative) + sound)

def rusanov(lower_state, upper_state, direction, mesh_speed):
    flux_low, speed_low = euler_flux(lower_state, direction, mesh_speed)
    flux_high, speed_high = euler_flux(upper_state, direction, mesh_speed)
    return 0.5 * (flux_low + flux_high) - 0.5 * jnp.maximum(speed_low, speed_high) * (upper_state - lower_state)

def face_rates(conserved, x_lower, x_upper, y_lower, y_upper, scale_x, scale_y, scale_z, faces_x, faces_y, faces_z):
    nodes, weights, deriv = lgl_tables()
    tile_x, tile_y, column = (conserved.shape[4], conserved.shape[5], conserved.shape[6])
    deriv_mat = jnp.asarray(deriv, jnp.float32)
    lower_half = jnp.asarray((1.0 - nodes) / 2.0, jnp.float32)
    upper_half = jnp.asarray((1.0 + nodes) / 2.0, jnp.float32)
    first_w = float(weights[0])
    last_w = float(weights[3])
    exact = lax.Precision.HIGHEST
    node_x = (faces_x[None, :-1] * lower_half[:, None] + faces_x[None, 1:] * upper_half[:, None]).reshape(4, 1, 1, tile_x, 1, 1)
    flux_x = euler_flux(conserved, 0, node_x)[0]
    grad_x = jnp.einsum('pa,vabcijk->vpbcijk', deriv_mat, flux_x, precision=exact)
    star_x = rusanov(jnp.concatenate([x_lower, conserved[:, 3]], axis=3), jnp.concatenate([conserved[:, 0], x_upper], axis=3), 0, faces_x.reshape(1, 1, tile_x + 1, 1, 1))
    low_x = star_x[:, :, :, :-1]
    high_x = star_x[:, :, :, 1:]
    blank_x = jnp.zeros_like(low_x)
    dg_x = -scale_x * (grad_x + jnp.stack([-(low_x - flux_x[:, 0]) / first_w, blank_x, blank_x, (high_x - flux_x[:, 3]) / last_w], axis=1))
    fv_x = scale_x * jnp.stack([low_x / first_w, blank_x, blank_x, -high_x / last_w], axis=1)
    node_y = (faces_y[None, :-1] * lower_half[:, None] + faces_y[None, 1:] * upper_half[:, None]).reshape(1, 4, 1, 1, tile_y, 1)
    flux_y = euler_flux(conserved, 1, node_y)[0]
    grad_y = jnp.einsum('pb,vabcijk->vapcijk', deriv_mat, flux_y, precision=exact)
    star_y = rusanov(jnp.concatenate([y_lower, conserved[:, :, 3]], axis=4), jnp.concatenate([conserved[:, :, 0], y_upper], axis=4), 1, faces_y.reshape(1, 1, 1, tile_y + 1, 1))
    low_y = star_y[:, :, :, :, :-1]
    high_y = star_y[:, :, :, :, 1:]
    blank_y = jnp.zeros_like(low_y)
    dg_y = -scale_y * (grad_y + jnp.stack([-(low_y - flux_y[:, :, 0]) / first_w, blank_y, blank_y, (high_y - flux_y[:, :, 3]) / last_w], axis=2))
    fv_y = scale_y * jnp.stack([low_y / first_w, blank_y, blank_y, -high_y / last_w], axis=2)
    next_z = jnp.roll(faces_z, -1)
    node_z = (faces_z[None, :] * lower_half[:, None] + next_z[None, :] * upper_half[:, None]).reshape(1, 1, 4, 1, 1, column)
    flux_z = euler_flux(conserved, 2, node_z)[0]
    grad_z = jnp.einsum('pc,vabcijk->vabpijk', deriv_mat, flux_z, precision=exact)
    star_z = rusanov(jnp.roll(conserved[:, :, :, 3], 1, axis=5), conserved[:, :, :, 0], 2, faces_z.reshape(1, 1, 1, 1, column))
    low_z = star_z
    high_z = jnp.roll(star_z, -1, axis=5)
    blank_z = jnp.zeros_like(low_z)
    dg_z = -scale_z * (grad_z + jnp.stack([-(low_z - flux_z[:, :, :, 0]) / first_w, blank_z, blank_z, (high_z - flux_z[:, :, :, 3]) / last_w], axis=3))
    fv_z = scale_z * jnp.stack([low_z / first_w, blank_z, blank_z, -high_z / last_w], axis=3)
    return (dg_x + dg_y + dg_z, fv_x + fv_y + fv_z)

def fv_interior(conserved, scale_x, scale_y, scale_z, low_x, high_x, low_y, high_y, low_z, high_z):
    nodes, weights, deriv = lgl_tables()
    interfaces_xi = (-5.0 / 6.0, 0.0, 5.0 / 6.0)

    def direction_rate(direction, lower_speed, upper_speed):
        fluxes = []
        for interface in range(3):
            speed_here = lower_speed * ((1.0 - interfaces_xi[interface]) / 2.0) + upper_speed * ((1.0 + interfaces_xi[interface]) / 2.0)
            left_state = lax.index_in_dim(conserved, interface, direction + 1, keepdims=False)
            right_state = lax.index_in_dim(conserved, interface + 1, direction + 1, keepdims=False)
            fluxes.append(rusanov(left_state, right_state, direction, speed_here))
        jumps = jnp.stack([fluxes[0], fluxes[1] - fluxes[0], fluxes[2] - fluxes[1], -fluxes[2]], axis=direction + 1)
        shaped = [1] * conserved.ndim
        shaped[direction + 1] = 4
        return jumps / jnp.asarray(weights, jnp.float32).reshape(shaped)
    return -scale_x * direction_rate(0, low_x, high_x) - scale_y * direction_rate(1, low_y, high_y) - scale_z * direction_rate(2, low_z, high_z)

def corner_hessian(density, inv_x, inv_y, inv_z):
    nodes, weights, deriv = lgl_tables()
    first_order = jnp.asarray(deriv[[0, 3]], jnp.float32)
    second_order = jnp.asarray((deriv @ deriv)[[0, 3]], jnp.float32)
    select_rows = jnp.asarray(np.eye(4)[[0, 3]], jnp.float32)

    def contract(along_a, along_b, along_c):
        return jnp.einsum('pa,qb,rc,abcijk->pqrijk', along_a, along_b, along_c, density, precision=lax.Precision.HIGHEST)
    return jnp.stack([contract(second_order, select_rows, select_rows) * inv_x * inv_x, contract(select_rows, second_order, select_rows) * inv_y * inv_y, contract(select_rows, select_rows, second_order) * inv_z * inv_z, contract(first_order, first_order, select_rows) * inv_x * inv_y, contract(first_order, select_rows, first_order) * inv_x * inv_z, contract(select_rows, first_order, first_order) * inv_y * inv_z])

def reference(conserved, troubled_list, widths_x, widths_y, widths_z, speed_x, speed_y, speed_z):
    count_x = widths_x.shape[0]
    count_y = widths_y.shape[0]
    column = widths_z.shape[0]
    local_count = EX * EY * EZ
    devices = N_GX * N_GY
    listed = troubled_list.reshape(devices, 2 * BAL)
    owners = jnp.broadcast_to(jnp.arange(devices, dtype=jnp.int32)[:, None], listed.shape)
    marks = jnp.zeros((devices, local_count), bool).at[owners, listed].set(True, mode='drop')
    marks = marks.reshape(N_GX, N_GY, EX, EY, EZ).transpose(0, 2, 1, 3, 4).reshape(count_x, count_y, column)
    next_x = jnp.roll(speed_x, -1)
    new_x = widths_x + time_step * (next_x - speed_x)
    new_y = widths_y + time_step * (jnp.roll(speed_y, -1) - speed_y)
    new_z = widths_z + time_step * (jnp.roll(speed_z, -1) - speed_z)
    faces_y = jnp.concatenate([speed_y, speed_y[:1]])
    scale_y = (2.0 / widths_y).reshape(1, count_y, 1)
    scale_z = (2.0 / widths_z).reshape(1, 1, column)
    low_y = speed_y.reshape(1, count_y, 1)
    high_y = faces_y[1:].reshape(1, count_y, 1)
    low_z = speed_z.reshape(1, 1, column)
    high_z = jnp.roll(speed_z, -1).reshape(1, 1, column)

    def slab(index_x):
        current = lax.dynamic_slice_in_dim(conserved, index_x, 1, 4)
        x_lower = lax.dynamic_slice_in_dim(conserved, (index_x + count_x - 1) % count_x, 1, 4)[:, 3]
        x_upper = lax.dynamic_slice_in_dim(conserved, (index_x + 1) % count_x, 1, 4)[:, 0]
        y_lower = current[:, :, 3][:, :, :, :, -1:]
        y_upper = current[:, :, 0][:, :, :, :, 0:1]
        width_here = lax.dynamic_slice_in_dim(widths_x, index_x, 1)
        faces_x = jnp.concatenate([lax.dynamic_slice_in_dim(speed_x, index_x, 1), lax.dynamic_slice_in_dim(next_x, index_x, 1)])
        scale_x = (2.0 / width_here).reshape(1, 1, 1)
        dg_rate, fv_face = face_rates(current, x_lower, x_upper, y_lower, y_upper, scale_x, scale_y, scale_z, faces_x, faces_y, speed_z)
        inner = fv_interior(current, scale_x, scale_y, scale_z, faces_x[0:1].reshape(1, 1, 1), faces_x[1:2].reshape(1, 1, 1), low_y, high_y, low_z, high_z)
        troubled = lax.dynamic_slice_in_dim(marks, index_x, 1, 0)
        rate = jnp.where(troubled, fv_face + inner, dg_rate)
        new_here = lax.dynamic_slice_in_dim(new_x, index_x, 1)
        ratio = width_here.reshape(1, 1, 1) * widths_y.reshape(1, count_y, 1) * widths_z.reshape(1, 1, column) / (new_here.reshape(1, 1, 1) * new_y.reshape(1, count_y, 1) * new_z.reshape(1, 1, column))
        return (ratio * (current + time_step * rate))[:, :, :, :, 0]
    advanced = jnp.moveaxis(lax.map(slab, jnp.arange(count_x, dtype=jnp.int32)), 0, 4)
    inv_x = (2.0 / new_x).reshape(count_x, 1, 1)
    inv_y = (2.0 / new_y).reshape(1, count_y, 1)
    inv_z = (2.0 / new_z).reshape(1, 1, column)
    mass = new_x.reshape(count_x, 1, 1) * new_y.reshape(1, count_y, 1) * new_z.reshape(1, 1, column)
    weighted = corner_hessian(advanced[0], inv_x, inv_y, inv_z) * mass
    totals = jnp.zeros((6, count_x, count_y, column), jnp.float32)
    for side_x in (0, 1):
        for side_y in (0, 1):
            for side_z in (0, 1):
                totals = totals + jnp.roll(weighted[:, side_x, side_y, side_z], (side_x, side_y, side_z), axis=(1, 2, 3))
    denominator = (new_x + jnp.roll(new_x, 1)).reshape(count_x, 1, 1) * (new_y + jnp.roll(new_y, 1)).reshape(1, count_y, 1) * (new_z + jnp.roll(new_z, 1)).reshape(1, 1, column)
    return (advanced, totals / denominator)
```

```python
import functools

import jax
import jax.numpy as jnp
import numpy as np
from jax import lax
from jax.experimental import pallas as pl
from jax.experimental.pallas import tpu as pltpu
from jax.sharding import PartitionSpec as P

MESH = pl.DeviceIdType.MESH
time_step = 0.05
gamma_ratio = 1.4


def lgl_tables():
    nodes = np.array([-1.0, -1.0 / np.sqrt(5.0), 1.0 / np.sqrt(5.0), 1.0])
    weights = np.array([1.0 / 6.0, 5.0 / 6.0, 5.0 / 6.0, 1.0 / 6.0])
    barycentric = np.ones(4)
    for row_a in range(4):
        for row_b in range(4):
            if row_a != row_b:
                barycentric[row_a] = barycentric[row_a] / (nodes[row_a] - nodes[row_b])
    deriv = np.zeros((4, 4))
    for row_a in range(4):
        for row_b in range(4):
            if row_a != row_b:
                deriv[row_a, row_b] = (
                    barycentric[row_b] / barycentric[row_a] / (nodes[row_a] - nodes[row_b])
                )
    for row_a in range(4):
        deriv[row_a, row_a] = -np.sum(deriv[row_a])
    return (nodes, weights, deriv)


NODES, WEIGHTS, DERIV = lgl_tables()
SPEED, INTER, SCALE, FACE = 0, 12, 21, 27
RATIO, MASK, GEO = 33, 34, 35


def primitives(state):
    inverse = 1.0 / state[0]
    square = state[1] * state[1] + state[2] * state[2] + state[3] * state[3]
    pressure = (gamma_ratio - 1.0) * (state[4] - 0.5 * square * inverse)
    ratio = gamma_ratio * pressure * inverse
    return inverse, pressure, ratio * lax.rsqrt(ratio)


def twice_flux(low, p_low, c_low, u_low, high, p_high, c_high, u_high, direction, speed):
    rel_low = u_low - speed
    rel_high = u_high - speed
    fastest = jnp.maximum(jnp.abs(rel_low) + c_low, jnp.abs(rel_high) + c_high)
    left = rel_low + fastest
    right = rel_high - fastest
    flux = [low[v] * left + high[v] * right for v in range(5)]
    flux[direction + 1] = flux[direction + 1] + (p_low + p_high)
    flux[4] = flux[4] + (p_low * u_low + p_high * u_high)
    return flux


def dg_apply(values):
    lifted = DERIV.copy()
    lifted[0, 0] += 1.0 / WEIGHTS[0]
    lifted[3, 3] -= 1.0 / WEIGHTS[3]
    lifted = 2.0 * WEIGHTS[:, None] * lifted
    odd_0, odd_1 = values[0] - values[3], values[1] - values[2]
    even_0, even_1 = values[0] + values[3], values[1] + values[2]
    out = [None] * 4
    for row in (0, 1):
        total = 0.5 * (lifted[row, 0] - lifted[row, 3]) * odd_0
        total = total + 0.5 * (lifted[row, 1] - lifted[row, 2]) * odd_1
        apart = 0.5 * (lifted[row, 0] + lifted[row, 3]) * even_0
        apart = apart + 0.5 * (lifted[row, 1] + lifted[row, 2]) * even_1
        out[row] = total + apart
        out[3 - row] = total - apart
    return out


def kernel(
    tile_x,
    tile_y,
    sizes,
    cons_hbm,
    list_ref,
    wx_ref,
    wy_ref,
    wz_ref,
    sx_ref,
    sy_ref,
    sz_ref,
    adv_hbm,
    hess_ref,
    state,
    out,
    inv_s,
    pres_s,
    sound_s,
    geo,
    xs,
    xr,
    ys,
    yr,
    rxs,
    rxr,
    rys,
    ryr,
    rds,
    rdr,
    io_sem,
    send_sem,
    recv_sem,
):
    size_x, size_y = sizes
    rows = tile_x * tile_y
    lanes = state.shape[-1]
    me_x, me_y = lax.axis_index("gx"), lax.axis_index("gy")
    up_x, down_x = lax.rem(me_x + 1, size_x), lax.rem(me_x + size_x - 1, size_x)
    up_y, down_y = lax.rem(me_y + 1, size_y), lax.rem(me_y + size_y - 1, size_y)

    load = pltpu.make_async_copy(cons_hbm, state, io_sem.at[0])
    load.start()
    barrier = pltpu.get_barrier_semaphore()
    partners = (
        (up_x, me_y),
        (down_x, me_y),
        (me_x, up_y),
        (me_x, down_y),
        (up_x, up_y),
        (down_x, down_y),
    )
    for partner in partners:
        pl.semaphore_signal(barrier, inc=1, device_id=partner, device_id_type=MESH)

    shape = (rows, lanes)
    row = lax.broadcasted_iota(jnp.int32, shape, 0)
    row_i, row_j = row // tile_y, row % tile_y

    def roll_rows(value, shift):
        shift = shift % rows
        return value if shift == 0 else pltpu.roll(value, shift, 0)

    def roll_lanes(value, shift):
        return pltpu.roll(value, shift % lanes, 1)

    def along(ref, start, total, tile, index):
        values = [ref[lax.rem(start + total + i, total)] for i in range(-1, tile + 1)]

        def pick(offset):
            vector = jnp.full(shape, values[1 + offset], jnp.float32)
            for i in range(1, tile):
                vector = jnp.where(index == i, values[1 + offset + i], vector)
            return vector

        return pick(-1), pick(0), pick(1)

    total_x, total_y = size_x * tile_x, size_y * tile_y
    wx_p, wx, _ = along(wx_ref, me_x * tile_x, total_x, tile_x, row_i)
    wy_p, wy, _ = along(wy_ref, me_y * tile_y, total_y, tile_y, row_j)
    sx_p, sx, sx_n = along(sx_ref, me_x * tile_x, total_x, tile_x, row_i)
    sy_p, sy, sy_n = along(sy_ref, me_y * tile_y, total_y, tile_y, row_j)
    wz = jnp.broadcast_to(wz_ref[...], shape)
    sz = jnp.broadcast_to(sz_ref[...], shape)
    sz_n = roll_lanes(sz, -1)
    nx, ny, nz = (
        wx + time_step * (sx_n - sx),
        wy + time_step * (sy_n - sy),
        wz + time_step * (sz_n - sz),
    )
    px, py = wx_p + time_step * (sx - sx_p), wy_p + time_step * (sy - sy_p)
    pz = roll_lanes(nz, 1)
    mass = nx * ny * nz
    ratio = wx * wy * wz / mass
    geo[RATIO] = ratio
    for d, (width, low, high) in enumerate(((wx, sx, sx_n), (wy, sy, sy_n), (wz, sz, sz_n))):
        for a in range(4):
            geo[SPEED + 4 * d + a] = low * float((1.0 - NODES[a]) / 2.0) + high * float(
                (1.0 + NODES[a]) / 2.0
            )
        for q, xi in enumerate((-5.0 / 6.0, 0.0, 5.0 / 6.0)):
            geo[INTER + 3 * d + q] = low * ((1.0 - xi) / 2.0) + high * ((1.0 + xi) / 2.0)
        geo[FACE + 2 * d] = low
        geo[FACE + 2 * d + 1] = high
        kappa = -time_step * ratio / width
        geo[SCALE + 2 * d] = kappa * float(1.0 / WEIGHTS[0])
        geo[SCALE + 2 * d + 1] = kappa * float(1.0 / WEIGHTS[1])

    entries = list_ref[...]
    count = entries.shape[-1]
    in_row = jnp.where(
        lax.broadcasted_iota(jnp.int32, (rows, count), 0) == entries // lanes, 1.0, 0.0
    )
    in_lane = jnp.where(
        lax.broadcasted_iota(jnp.int32, (lanes, count), 0) == entries % lanes, 1.0, 0.0
    )
    geo[MASK] = lax.dot_general(
        in_row, in_lane, (((1,), (1,)), ((), ())), preferred_element_type=jnp.float32
    )

    load.wait()

    def pack_faces(q, carry):
        for v in range(5):
            for side, node, first in ((0, 0, 0), (1, 3, rows - tile_y)):
                packed = None
                for c in range(4):
                    part = roll_rows(state[v, node, q, c], tile_y * c - first)
                    packed = part if packed is None else jnp.where(row_i == c, part, packed)
                xs[side, v, q] = packed
            for side, node, first in ((0, 0, 0), (1, 3, tile_y - 1)):
                for group in range(4 // tile_y):
                    packed = None
                    for c in range(tile_y):
                        part = roll_rows(state[v, q, node, group * tile_y + c], c - first)
                        packed = part if packed is None else jnp.where(row_j == c, part, packed)
                    ys[side, v, q, group] = packed
        return carry

    lax.fori_loop(0, 4, pack_faces, 0)
    pl.semaphore_wait(barrier, len(partners))

    def remote(src, dst, slot, device):
        return pltpu.make_async_remote_copy(
            src_ref=src,
            dst_ref=dst,
            send_sem=send_sem.at[slot],
            recv_sem=recv_sem.at[slot],
            device_id=device,
            device_id_type=MESH,
        )

    faces = [
        remote(ys.at[0], yr.at[1], 2, (me_x, down_y)),
        remote(ys.at[1], yr.at[0], 3, (me_x, up_y)),
        remote(xs.at[0], xr.at[1], 0, (down_x, me_y)),
        remote(xs.at[1], xr.at[0], 1, (up_x, me_y)),
    ]
    for copy in faces:
        copy.start()

    def prepare(index, carry):
        a, b = index // 4, index % 4
        for c in range(4):
            inverse, pressure, sound = primitives([state[v, a, b, c] for v in range(5)])
            inv_s[a, b, c] = inverse
            pres_s[a, b, c] = pressure
            sound_s[a, b, c] = sound
        return carry

    lax.fori_loop(0, 16, prepare, 0)

    def interior(d, index, carry):
        first, second = index // 4, index % 4

        def at(n):
            return ((n, first, second), (first, n, second), (first, second, n))[d]

        mask = geo[MASK] > 0.5
        states = [[state[(v,) + at(n)] for v in range(5)] for n in range(4)]
        pressure = [pres_s[at(n)] for n in range(4)]
        sound = [sound_s[at(n)] for n in range(4)]
        normal = [states[n][d + 1] * inv_s[at(n)] for n in range(4)]
        inner = [
            twice_flux(
                states[q],
                pressure[q],
                sound[q],
                normal[q],
                states[q + 1],
                pressure[q + 1],
                sound[q + 1],
                normal[q + 1],
                d,
                geo[INTER + 3 * d + q],
            )
            for q in range(3)
        ]
        relative = [normal[n] - geo[SPEED + 4 * d + n] for n in range(4)]
        if d == 2:
            star_low = twice_flux(
                [roll_lanes(states[3][v], 1) for v in range(5)],
                roll_lanes(pressure[3], 1),
                roll_lanes(sound[3], 1),
                roll_lanes(normal[3], 1),
                states[0],
                pressure[0],
                sound[0],
                normal[0],
                d,
                geo[FACE + 2 * d],
            )
        for v in range(5):
            flux = [states[n][v] * relative[n] for n in range(4)]
            if v == d + 1:
                flux = [flux[n] + pressure[n] for n in range(4)]
            if v == 4:
                flux = [flux[n] + pressure[n] * normal[n] for n in range(4)]
            smooth = dg_apply(flux)
            fv = [inner[0][v], inner[1][v] - inner[0][v], inner[2][v] - inner[1][v], -inner[2][v]]
            chosen = [jnp.where(mask, fv[n], smooth[n]) for n in range(4)]
            if d == 2:
                chosen[0] = chosen[0] - star_low[v]
                chosen[3] = chosen[3] + roll_lanes(star_low[v], -1)
            for n in range(4):
                where = (v,) + at(n)
                scale = geo[SCALE + 2 * d + (0 if n in (0, 3) else 1)]
                if d == 0:
                    base = geo[RATIO] * states[n][v]
                else:
                    base = out[where]
                out[where] = base + scale * chosen[n]
        return carry

    for d in range(3):
        lax.fori_loop(0, 16, functools.partial(interior, d), 0)

    def surface(d, q, carry):
        for c in range(4):
            at = ((lambda n: (n, q, c)), (lambda n: (q, n, c)))[d]
            scale = geo[SCALE + 2 * d]
            shift = (tile_y, 1)[d]
            edge = (row_i, row_j)[d]
            last = (tile_x, tile_y)[d] - 1
            for side, node, far in ((0, 0, 3), (1, 3, 0)):
                own = [state[(v,) + at(node)] for v in range(5)]
                other = []
                for v in range(5):
                    if d == 0:
                        to = 0 if side == 0 else rows - tile_y
                        halo = roll_rows(xr[side, v, q], to - tile_y * c)
                    else:
                        to = 0 if side == 0 else tile_y - 1
                        halo = roll_rows(yr[side, v, q, c // tile_y], to - c % tile_y)
                    moved = roll_rows(state[(v,) + at(far)], shift if side == 0 else -shift)
                    other.append(jnp.where(edge == (0 if side == 0 else last), halo, moved))
                inverse, pressure, sound = primitives(other)
                own_side = (
                    own,
                    pres_s[at(node)],
                    sound_s[at(node)],
                    own[d + 1] * inv_s[at(node)],
                )
                other_side = (other, pressure, sound, other[d + 1] * inverse)
                low, high = (other_side, own_side) if side == 0 else (own_side, other_side)
                star = twice_flux(*low, *high, d, geo[FACE + 2 * d + side])
                for v in range(5):
                    where = (v,) + at(node)
                    if side == 0:
                        out[where] = out[where] - scale * star[v]
                    else:
                        out[where] = out[where] + scale * star[v]
        return carry

    faces[2].wait()
    faces[3].wait()
    lax.fori_loop(0, 4, functools.partial(surface, 0), 0)
    faces[0].wait()
    faces[1].wait()
    lax.fori_loop(0, 4, functools.partial(surface, 1), 0)

    store = pltpu.make_async_copy(out, adv_hbm, io_sem.at[1])
    store.start()

    second = DERIV @ DERIV
    ends = (0, 3)

    def combine(coefficients, values):
        total = float(coefficients[0]) * values[0]
        for n in range(1, 4):
            total = total + float(coefficients[n]) * values[n]
        return total

    density = [[[out[0, a, b, c] for c in range(4)] for b in range(4)] for a in range(4)]
    ix, iy, iz = 2.0 / nx, 2.0 / ny, 2.0 / nz
    factors = (
        mass * ix * ix,
        mass * iy * iy,
        mass * iz * iz,
        mass * ix * iy,
        mass * ix * iz,
        mass * iy * iz,
    )
    along_x = {
        (p, b, c): combine(DERIV[p], [density[a][b][c] for a in range(4)])
        for p in ends
        for b in range(4)
        for c in range(4)
        if b in ends or c in ends
    }
    along_y = {
        (a, q, c): combine(DERIV[q], [density[a][b][c] for b in range(4)])
        for q in ends
        for a in ends
        for c in range(4)
    }

    def corner(kind, p, q, r):
        if kind == 0:
            return combine(second[p], [density[a][q][r] for a in range(4)])
        if kind == 1:
            return combine(second[q], [density[p][b][r] for b in range(4)])
        if kind == 2:
            return combine(second[r], [density[p][q][c] for c in range(4)])
        if kind == 3:
            return combine(DERIV[q], [along_x[p, b, r] for b in range(4)])
        if kind == 4:
            return combine(DERIV[r], [along_x[p, q, c] for c in range(4)])
        return combine(DERIV[r], [along_y[p, q, c] for c in range(4)])

    own_sum = []
    x_rim = [None] * -(-6 // tile_x)
    y_rim = [None] * -(-6 // tile_y)
    d_rim = None
    for kind in range(6):
        column = {}
        for p in ends:
            for q in ends:
                low = factors[kind] * corner(kind, p, q, 0)
                high = factors[kind] * corner(kind, p, q, 3)
                column[p, q] = low + roll_lanes(high, 1)
        def up_y_shift(value):
            return jnp.where(row_j == 0, 0.0, roll_rows(value, 1))

        low_x = column[0, 0] + up_y_shift(column[0, 3])
        high_x = column[3, 0] + up_y_shift(column[3, 3])
        moved = jnp.where(row_i == 0, 0.0, roll_rows(high_x, tile_y))
        own_sum.append(low_x + moved)
        slot, place = kind // tile_x, kind % tile_x
        part = roll_rows(high_x, tile_y * place - (rows - tile_y))
        x_rim[slot] = part if place == 0 else jnp.where(row_i == place, part, x_rim[slot])
        rim = column[0, 3] + jnp.where(row_i == 0, 0.0, roll_rows(column[3, 3], tile_y))
        slot, place = kind // tile_y, kind % tile_y
        part = roll_rows(rim, place - (tile_y - 1))
        y_rim[slot] = part if place == 0 else jnp.where(row_j == place, part, y_rim[slot])
        part = roll_rows(column[3, 3], kind - (rows - 1))
        d_rim = part if kind == 0 else jnp.where(row == kind, part, d_rim)
    for slot, value in enumerate(x_rim):
        rxs[slot] = value
    for slot, value in enumerate(y_rim):
        rys[slot] = value
    rds[...] = d_rim
    rims = [
        remote(rds, rdr, 6, (up_x, up_y)),
        remote(rys, ryr, 5, (me_x, up_y)),
        remote(rxs, rxr, 4, (up_x, me_y)),
    ]
    for copy in rims:
        copy.start()
    inverse = 1.0 / ((nx + px) * (ny + py) * (nz + pz))
    for kind in range(6):
        hess_ref[kind] = own_sum[kind]
    for copy in rims:
        copy.wait()
    for kind in range(6):
        total = hess_ref[kind]
        from_x = roll_rows(rxr[kind // tile_x], -tile_y * (kind % tile_x))
        total = total + jnp.where(row_i == 0, from_x, 0.0)
        from_y = roll_rows(ryr[kind // tile_y], -(kind % tile_y))
        total = total + jnp.where(row_j == 0, from_y, 0.0)
        total = total + jnp.where(row == 0, roll_rows(rdr[...], -kind), 0.0)
        hess_ref[kind] = total * inverse
    store.wait()


def solution(mesh):
    sizes = (mesh.shape["gx"], mesh.shape["gy"])

    def local(conserved, troubled_list, widths_x, widths_y, widths_z, speed_x, speed_y, speed_z):
        tile_x, tile_y, column = conserved.shape[4:]
        rows = tile_x * tile_y
        f32 = jnp.float32
        smem = pl.BlockSpec(memory_space=pltpu.SMEM)
        vmem = pl.BlockSpec(memory_space=pltpu.VMEM)
        whole = pl.BlockSpec(memory_space=pl.ANY)
        full = (5, 4, 4, 4, rows, column)
        nodal = (4, 4, 4, rows, column)
        x_face = (2, 5, 4, rows, column)
        y_face = (2, 5, 4, 4 // tile_y, rows, column)
        x_rim = (-(-6 // tile_x), rows, column)
        y_rim = (-(-6 // tile_y), rows, column)
        advanced, hessian = pl.pallas_call(
            functools.partial(kernel, tile_x, tile_y, sizes),
            out_shape=(
                jax.ShapeDtypeStruct(full, f32),
                jax.ShapeDtypeStruct((6, rows, column), f32),
            ),
            in_specs=[whole, vmem, smem, smem, vmem, smem, smem, vmem],
            out_specs=(whole, vmem),
            scratch_shapes=[
                pltpu.VMEM(full, f32),
                pltpu.VMEM(full, f32),
                pltpu.VMEM(nodal, f32),
                pltpu.VMEM(nodal, f32),
                pltpu.VMEM(nodal, f32),
                pltpu.VMEM((GEO, rows, column), f32),
                pltpu.VMEM(x_face, f32),
                pltpu.VMEM(x_face, f32),
                pltpu.VMEM(y_face, f32),
                pltpu.VMEM(y_face, f32),
                pltpu.VMEM(x_rim, f32),
                pltpu.VMEM(x_rim, f32),
                pltpu.VMEM(y_rim, f32),
                pltpu.VMEM(y_rim, f32),
                pltpu.VMEM((rows, column), f32),
                pltpu.VMEM((rows, column), f32),
                pltpu.SemaphoreType.DMA((2,)),
                pltpu.SemaphoreType.DMA((7,)),
                pltpu.SemaphoreType.DMA((7,)),
            ],
            compiler_params=pltpu.CompilerParams(collective_id=0, has_side_effects=True),
        )(
            conserved.reshape(full),
            troubled_list.reshape(1, -1),
            widths_x,
            widths_y,
            widths_z.reshape(1, -1),
            speed_x,
            speed_y,
            speed_z.reshape(1, -1),
        )
        return advanced.reshape(conserved.shape), hessian.reshape(6, tile_x, tile_y, column)

    in_specs = (
        P(None, None, None, None, "gx", "gy", None),
        P(("gx", "gy")),
        P(),
        P(),
        P(),
        P(),
        P(),
        P(),
    )
    out_specs = (P(None, None, None, None, "gx", "gy", None), P(None, "gx", "gy", None))
    return jax.shard_map(local, mesh=mesh, in_specs=in_specs, out_specs=out_specs, check_vma=False)
```

```python
import functools

import jax
import jax.numpy as jnp
import numpy as np
from jax import lax
from jax.experimental import pallas as pl
from jax.experimental.pallas import tpu as pltpu
from jax.sharding import PartitionSpec as P

MESH = pl.DeviceIdType.MESH
time_step = 0.05
gamma_ratio = 1.4


def lgl_tables():
    nodes = np.array([-1.0, -1.0 / np.sqrt(5.0), 1.0 / np.sqrt(5.0), 1.0])
    weights = np.array([1.0 / 6.0, 5.0 / 6.0, 5.0 / 6.0, 1.0 / 6.0])
    barycentric = np.ones(4)
    for row_a in range(4):
        for row_b in range(4):
            if row_a != row_b:
                barycentric[row_a] = barycentric[row_a] / (nodes[row_a] - nodes[row_b])
    deriv = np.zeros((4, 4))
    for row_a in range(4):
        for row_b in range(4):
            if row_a != row_b:
                deriv[row_a, row_b] = (
                    barycentric[row_b] / barycentric[row_a] / (nodes[row_a] - nodes[row_b])
                )
    for row_a in range(4):
        deriv[row_a, row_a] = -np.sum(deriv[row_a])
    return (nodes, weights, deriv)


NODES, WEIGHTS, DERIV = lgl_tables()
SPEED, INTER, SCALE, FACE = 0, 12, 21, 27
RATIO, MASK, GEO = 33, 34, 35
ALL, DENSITY, REST = (0, 1, 2, 3, 4), (0,), (1, 2, 3, 4)
FIRST = ((0, ALL), (1, ALL), (2, DENSITY))
LATER = ((2, REST),)


def primitives(state):
    inverse = 1.0 / state[0]
    square = state[1] * state[1] + state[2] * state[2] + state[3] * state[3]
    pressure = (gamma_ratio - 1.0) * (state[4] - 0.5 * square * inverse)
    ratio = gamma_ratio * pressure * inverse
    return inverse, pressure, ratio * lax.rsqrt(ratio)


def twice_flux(low, p_low, c_low, u_low, high, p_high, c_high, u_high, direction, speed):
    rel_low = u_low - speed
    rel_high = u_high - speed
    fastest = jnp.maximum(jnp.abs(rel_low) + c_low, jnp.abs(rel_high) + c_high)
    left = rel_low + fastest
    right = rel_high - fastest
    flux = [low[v] * left + high[v] * right for v in range(5)]
    flux[direction + 1] = flux[direction + 1] + (p_low + p_high)
    flux[4] = flux[4] + (p_low * u_low + p_high * u_high)
    return flux


def dg_apply(values):
    lifted = DERIV.copy()
    lifted[0, 0] += 1.0 / WEIGHTS[0]
    lifted[3, 3] -= 1.0 / WEIGHTS[3]
    lifted = 2.0 * WEIGHTS[:, None] * lifted
    odd_0, odd_1 = values[0] - values[3], values[1] - values[2]
    even_0, even_1 = values[0] + values[3], values[1] + values[2]
    out = [None] * 4
    for row in (0, 1):
        total = 0.5 * (lifted[row, 0] - lifted[row, 3]) * odd_0
        total = total + 0.5 * (lifted[row, 1] - lifted[row, 2]) * odd_1
        apart = 0.5 * (lifted[row, 0] + lifted[row, 3]) * even_0
        apart = apart + 0.5 * (lifted[row, 1] + lifted[row, 2]) * even_1
        out[row] = total + apart
        out[3 - row] = total - apart
    return out


def kernel(
    tile_x,
    tile_y,
    sizes,
    cons_hbm,
    list_hbm,
    wx_hbm,
    wy_hbm,
    wz_hbm,
    sx_hbm,
    sy_hbm,
    sz_hbm,
    out,
    hess_ref,
    list_ref,
    wx_ref,
    wy_ref,
    wz_ref,
    sx_ref,
    sy_ref,
    sz_ref,
    state,
    inv_s,
    pres_s,
    sound_s,
    geo,
    xs,
    xr,
    ys,
    yr,
    rxs,
    rxr,
    rys,
    ryr,
    rds,
    rdr,
    io_sem,
    send_sem,
    recv_sem,
):
    size_x, size_y = sizes
    rows = tile_x * tile_y
    lanes = state.shape[-1]
    me_x, me_y = lax.axis_index("gx"), lax.axis_index("gy")
    up_x, down_x = lax.rem(me_x + 1, size_x), lax.rem(me_x + size_x - 1, size_x)
    up_y, down_y = lax.rem(me_y + 1, size_y), lax.rem(me_y + size_y - 1, size_y)

    barrier = pltpu.get_barrier_semaphore()
    partners = ((me_x, down_y), (me_x, up_y), (down_x, me_y), (up_x, me_y))
    for partner in partners:
        pl.semaphore_signal(barrier, inc=1, device_id=partner, device_id_type=MESH)
    small = [
        pltpu.make_async_copy(src, dst, io_sem.at[4 + n])
        for n, (src, dst) in enumerate(
            (
                (wx_hbm, wx_ref),
                (wy_hbm, wy_ref),
                (sx_hbm, sx_ref),
                (sy_hbm, sy_ref),
                (wz_hbm, wz_ref),
                (sz_hbm, sz_ref),
                (list_hbm, list_ref),
            )
        )
    ]
    loads = [pltpu.make_async_copy(cons_hbm.at[:, a], state.at[:, a], io_sem.at[a]) for a in range(4)]
    for a in (0, 3, 1, 2):
        loads[a].start()
    for copy in small:
        copy.start()

    shape = (rows, lanes)
    row = lax.broadcasted_iota(jnp.int32, shape, 0)
    row_i, row_j = row // tile_y, row % tile_y

    def roll_rows(value, shift):
        shift = shift % rows
        return value if shift == 0 else pltpu.roll(value, shift, 0)

    def roll_lanes(value, shift):
        return pltpu.roll(value, shift % lanes, 1)

    def pack_x(q, carry):
        for v in range(5):
            for side, node, first in ((0, 0, 0), (1, 3, rows - tile_y)):
                packed = None
                for c in range(4):
                    part = roll_rows(state[v, node, q, c], tile_y * c - first)
                    packed = part if packed is None else jnp.where(row_i == c, part, packed)
                xs[side, v, q] = packed
        return carry

    def pack_y(q, carry):
        for v in range(5):
            for side, node, first in ((0, 0, 0), (1, 3, tile_y - 1)):
                for group in range(4 // tile_y):
                    packed = None
                    for c in range(tile_y):
                        part = roll_rows(state[v, q, node, group * tile_y + c], c - first)
                        packed = part if packed is None else jnp.where(row_j == c, part, packed)
                    ys[side, v, q, group] = packed
        return carry

    for a in (0, 3, 1, 2):
        loads[a].wait()
        pack_y(a, 0)
    pl.semaphore_wait(barrier, len(partners))

    def remote(src, dst, slot, device):
        return pltpu.make_async_remote_copy(
            src_ref=src,
            dst_ref=dst,
            send_sem=send_sem.at[slot],
            recv_sem=recv_sem.at[slot],
            device_id=device,
            device_id_type=MESH,
        )

    faces = [
        remote(ys.at[0], yr.at[1], 2, (me_x, down_y)),
        remote(ys.at[1], yr.at[0], 3, (me_x, up_y)),
        remote(xs.at[0], xr.at[1], 0, (down_x, me_y)),
        remote(xs.at[1], xr.at[0], 1, (up_x, me_y)),
    ]
    faces[0].start()
    faces[1].start()
    lax.fori_loop(0, 4, pack_x, 0)
    faces[2].start()
    faces[3].start()
    for copy in small:
        copy.wait()

    def along(ref, start, total, tile, index):
        values = [ref[lax.rem(start + total + i, total)] for i in range(-1, tile + 1)]

        def pick(offset):
            vector = jnp.full(shape, values[1 + offset], jnp.float32)
            for i in range(1, tile):
                vector = jnp.where(index == i, values[1 + offset + i], vector)
            return vector

        return pick(-1), pick(0), pick(1)

    total_x, total_y = size_x * tile_x, size_y * tile_y
    wx_p, wx, _ = along(wx_ref, me_x * tile_x, total_x, tile_x, row_i)
    wy_p, wy, _ = along(wy_ref, me_y * tile_y, total_y, tile_y, row_j)
    sx_p, sx, sx_n = along(sx_ref, me_x * tile_x, total_x, tile_x, row_i)
    sy_p, sy, sy_n = along(sy_ref, me_y * tile_y, total_y, tile_y, row_j)
    wz = jnp.broadcast_to(wz_ref[...], shape)
    sz = jnp.broadcast_to(sz_ref[...], shape)
    sz_n = roll_lanes(sz, -1)
    nx, ny, nz = (
        wx + time_step * (sx_n - sx),
        wy + time_step * (sy_n - sy),
        wz + time_step * (sz_n - sz),
    )
    px, py = wx_p + time_step * (sx - sx_p), wy_p + time_step * (sy - sy_p)
    pz = roll_lanes(nz, 1)
    mass = nx * ny * nz
    ratio = wx * wy * wz / mass
    geo[RATIO] = ratio
    for d, (width, low, high) in enumerate(((wx, sx, sx_n), (wy, sy, sy_n), (wz, sz, sz_n))):
        for a in range(4):
            geo[SPEED + 4 * d + a] = low * float((1.0 - NODES[a]) / 2.0) + high * float(
                (1.0 + NODES[a]) / 2.0
            )
        for q, xi in enumerate((-5.0 / 6.0, 0.0, 5.0 / 6.0)):
            geo[INTER + 3 * d + q] = low * ((1.0 - xi) / 2.0) + high * ((1.0 + xi) / 2.0)
        geo[FACE + 2 * d] = low
        geo[FACE + 2 * d + 1] = high
        kappa = -time_step * ratio / width
        geo[SCALE + 2 * d] = kappa * float(1.0 / WEIGHTS[0])
        geo[SCALE + 2 * d + 1] = kappa * float(1.0 / WEIGHTS[1])

    entries = list_ref[...]
    count = entries.shape[-1]
    in_row = jnp.where(
        lax.broadcasted_iota(jnp.int32, (rows, count), 0) == entries // lanes, 1.0, 0.0
    )
    in_lane = jnp.where(
        lax.broadcasted_iota(jnp.int32, (lanes, count), 0) == entries % lanes, 1.0, 0.0
    )
    geo[MASK] = lax.dot_general(
        in_row, in_lane, (((1,), (1,)), ((), ())), preferred_element_type=jnp.float32
    )

    def prepare(index, carry):
        a, b = index // 4, index % 4
        for c in range(4):
            inverse, pressure, sound = primitives([state[v, a, b, c] for v in range(5)])
            inv_s[a, b, c] = inverse
            pres_s[a, b, c] = pressure
            sound_s[a, b, c] = sound
        return carry

    lax.fori_loop(0, 16, prepare, 0)

    def interior(d, parts, index, carry):
        first, second = index // 4, index % 4

        def at(n):
            return ((n, first, second), (first, n, second), (first, second, n))[d]

        mask = geo[MASK] > 0.5
        states = [[state[(v,) + at(n)] for v in range(5)] for n in range(4)]
        pressure = [pres_s[at(n)] for n in range(4)]
        sound = [sound_s[at(n)] for n in range(4)]
        normal = [states[n][d + 1] * inv_s[at(n)] for n in range(4)]
        inner = [
            twice_flux(
                states[q],
                pressure[q],
                sound[q],
                normal[q],
                states[q + 1],
                pressure[q + 1],
                sound[q + 1],
                normal[q + 1],
                d,
                geo[INTER + 3 * d + q],
            )
            for q in range(3)
        ]
        relative = [normal[n] - geo[SPEED + 4 * d + n] for n in range(4)]
        if d == 2:
            star_low = twice_flux(
                [roll_lanes(states[3][v], 1) for v in range(5)],
                roll_lanes(pressure[3], 1),
                roll_lanes(sound[3], 1),
                roll_lanes(normal[3], 1),
                states[0],
                pressure[0],
                sound[0],
                normal[0],
                d,
                geo[FACE + 2 * d],
            )
        for v in parts:
            flux = [states[n][v] * relative[n] for n in range(4)]
            if v == d + 1:
                flux = [flux[n] + pressure[n] for n in range(4)]
            if v == 4:
                flux = [flux[n] + pressure[n] * normal[n] for n in range(4)]
            smooth = dg_apply(flux)
            fv = [inner[0][v], inner[1][v] - inner[0][v], inner[2][v] - inner[1][v], -inner[2][v]]
            chosen = [jnp.where(mask, fv[n], smooth[n]) for n in range(4)]
            if d == 2:
                chosen[0] = chosen[0] - star_low[v]
                chosen[3] = chosen[3] + roll_lanes(star_low[v], -1)
            for n in range(4):
                where = (v,) + at(n)
                scale = geo[SCALE + 2 * d + (0 if n in (0, 3) else 1)]
                if d == 0:
                    base = geo[RATIO] * states[n][v]
                else:
                    base = out[where]
                out[where] = base + scale * chosen[n]
        return carry

    for d, parts in FIRST:
        lax.fori_loop(0, 16, functools.partial(interior, d, parts), 0)

    def surface(d, parts, q, carry):
        for c in range(4):
            at = ((lambda n: (n, q, c)), (lambda n: (q, n, c)))[d]
            scale = geo[SCALE + 2 * d]
            shift = (tile_y, 1)[d]
            edge = (row_i, row_j)[d]
            last = (tile_x, tile_y)[d] - 1
            for side, node, far in ((0, 0, 3), (1, 3, 0)):
                own = [state[(v,) + at(node)] for v in range(5)]
                other = []
                for v in range(5):
                    if d == 0:
                        to = 0 if side == 0 else rows - tile_y
                        halo = roll_rows(xr[side, v, q], to - tile_y * c)
                    else:
                        to = 0 if side == 0 else tile_y - 1
                        halo = roll_rows(yr[side, v, q, c // tile_y], to - c % tile_y)
                    moved = roll_rows(state[(v,) + at(far)], shift if side == 0 else -shift)
                    other.append(jnp.where(edge == (0 if side == 0 else last), halo, moved))
                inverse, pressure, sound = primitives(other)
                own_side = (
                    own,
                    pres_s[at(node)],
                    sound_s[at(node)],
                    own[d + 1] * inv_s[at(node)],
                )
                other_side = (other, pressure, sound, other[d + 1] * inverse)
                low, high = (other_side, own_side) if side == 0 else (own_side, other_side)
                star = twice_flux(*low, *high, d, geo[FACE + 2 * d + side])
                for v in parts:
                    where = (v,) + at(node)
                    if side == 0:
                        out[where] = out[where] - scale * star[v]
                    else:
                        out[where] = out[where] + scale * star[v]
        return carry

    faces[2].wait()
    faces[3].wait()
    lax.fori_loop(0, 4, functools.partial(surface, 0, (0,)), 0)
    faces[0].wait()
    faces[1].wait()
    lax.fori_loop(0, 4, functools.partial(surface, 1, (0,)), 0)

    second = DERIV @ DERIV
    ends = (0, 3)

    def combine(coefficients, values):
        total = float(coefficients[0]) * values[0]
        for n in range(1, 4):
            total = total + float(coefficients[n]) * values[n]
        return total

    density = [[[out[0, a, b, c] for c in range(4)] for b in range(4)] for a in range(4)]
    ix, iy, iz = 2.0 / nx, 2.0 / ny, 2.0 / nz
    factors = (
        mass * ix * ix,
        mass * iy * iy,
        mass * iz * iz,
        mass * ix * iy,
        mass * ix * iz,
        mass * iy * iz,
    )
    along_x = {
        (p, b, c): combine(DERIV[p], [density[a][b][c] for a in range(4)])
        for p in ends
        for b in range(4)
        for c in range(4)
        if b in ends or c in ends
    }
    along_y = {
        (a, q, c): combine(DERIV[q], [density[a][b][c] for b in range(4)])
        for q in ends
        for a in ends
        for c in range(4)
    }

    def corner(kind, p, q, r):
        if kind == 0:
            return combine(second[p], [density[a][q][r] for a in range(4)])
        if kind == 1:
            return combine(second[q], [density[p][b][r] for b in range(4)])
        if kind == 2:
            return combine(second[r], [density[p][q][c] for c in range(4)])
        if kind == 3:
            return combine(DERIV[q], [along_x[p, b, r] for b in range(4)])
        if kind == 4:
            return combine(DERIV[r], [along_x[p, q, c] for c in range(4)])
        return combine(DERIV[r], [along_y[p, q, c] for c in range(4)])

    own_sum = []
    x_rim = [None] * -(-6 // tile_x)
    y_rim = [None] * -(-6 // tile_y)
    d_rim = None
    for kind in range(6):
        column = {}
        for p in ends:
            for q in ends:
                low = factors[kind] * corner(kind, p, q, 0)
                high = factors[kind] * corner(kind, p, q, 3)
                column[p, q] = low + roll_lanes(high, 1)
        def up_y_shift(value):
            return jnp.where(row_j == 0, 0.0, roll_rows(value, 1))

        low_x = column[0, 0] + up_y_shift(column[0, 3])
        high_x = column[3, 0] + up_y_shift(column[3, 3])
        moved = jnp.where(row_i == 0, 0.0, roll_rows(high_x, tile_y))
        own_sum.append(low_x + moved)
        slot, place = kind // tile_x, kind % tile_x
        part = roll_rows(high_x, tile_y * place - (rows - tile_y))
        x_rim[slot] = part if place == 0 else jnp.where(row_i == place, part, x_rim[slot])
        rim = column[0, 3] + jnp.where(row_i == 0, 0.0, roll_rows(column[3, 3], tile_y))
        slot, place = kind // tile_y, kind % tile_y
        part = roll_rows(rim, place - (tile_y - 1))
        y_rim[slot] = part if place == 0 else jnp.where(row_j == place, part, y_rim[slot])
        part = roll_rows(column[3, 3], kind - (rows - 1))
        d_rim = part if kind == 0 else jnp.where(row == kind, part, d_rim)
    for slot, value in enumerate(x_rim):
        rxs[slot] = value
    for slot, value in enumerate(y_rim):
        rys[slot] = value
    rds[...] = d_rim
    rims = [
        remote(rds, rdr, 6, (up_x, up_y)),
        remote(rys, ryr, 5, (me_x, up_y)),
        remote(rxs, rxr, 4, (up_x, me_y)),
    ]
    for copy in rims:
        copy.start()
    for d, parts in LATER:
        lax.fori_loop(0, 16, functools.partial(interior, d, parts), 0)
    for d in range(2):
        lax.fori_loop(0, 4, functools.partial(surface, d, (1, 2, 3, 4)), 0)
    inverse = 1.0 / ((nx + px) * (ny + py) * (nz + pz))
    for kind in range(6):
        hess_ref[kind] = own_sum[kind]
    for copy in rims:
        copy.wait()
    for kind in range(6):
        total = hess_ref[kind]
        from_x = roll_rows(rxr[kind // tile_x], -tile_y * (kind % tile_x))
        total = total + jnp.where(row_i == 0, from_x, 0.0)
        from_y = roll_rows(ryr[kind // tile_y], -(kind % tile_y))
        total = total + jnp.where(row_j == 0, from_y, 0.0)
        total = total + jnp.where(row == 0, roll_rows(rdr[...], -kind), 0.0)
        hess_ref[kind] = total * inverse


def emit(adv_ref, hess_ref, adv_out, hess_out, sem):
    copies = [
        pltpu.make_async_copy(adv_ref, adv_out, sem.at[0]),
        pltpu.make_async_copy(hess_ref, hess_out, sem.at[1]),
    ]
    for copy in copies:
        copy.start()
    for copy in copies:
        copy.wait()


def solution(mesh):
    sizes = (mesh.shape["gx"], mesh.shape["gy"])

    def local(conserved, troubled_list, widths_x, widths_y, widths_z, speed_x, speed_y, speed_z):
        tile_x, tile_y, column = conserved.shape[4:]
        rows = tile_x * tile_y
        f32 = jnp.float32
        vmem = pl.BlockSpec(memory_space=pltpu.VMEM)
        whole = pl.BlockSpec(memory_space=pl.ANY)
        full = (5, 4, 4, 4, rows, column)
        nodal = (4, 4, 4, rows, column)
        x_face = (2, 5, 4, rows, column)
        y_face = (2, 5, 4, 4 // tile_y, rows, column)
        x_rim = (-(-6 // tile_x), rows, column)
        y_rim = (-(-6 // tile_y), rows, column)
        advanced, hessian = pl.pallas_call(
            functools.partial(kernel, tile_x, tile_y, sizes),
            out_shape=(
                pltpu.VMEM(full, f32),
                pltpu.VMEM((6, rows, column), f32),
            ),
            in_specs=[whole] * 8,
            out_specs=(vmem, vmem),
            scratch_shapes=[
                pltpu.VMEM((1, troubled_list.shape[0]), jnp.int32),
                pltpu.SMEM(widths_x.shape, f32),
                pltpu.SMEM(widths_y.shape, f32),
                pltpu.VMEM((1, column), f32),
                pltpu.SMEM(speed_x.shape, f32),
                pltpu.SMEM(speed_y.shape, f32),
                pltpu.VMEM((1, column), f32),
                pltpu.VMEM(full, f32),
                pltpu.VMEM(nodal, f32),
                pltpu.VMEM(nodal, f32),
                pltpu.VMEM(nodal, f32),
                pltpu.VMEM((GEO, rows, column), f32),
                pltpu.VMEM(x_face, f32),
                pltpu.VMEM(x_face, f32),
                pltpu.VMEM(y_face, f32),
                pltpu.VMEM(y_face, f32),
                pltpu.VMEM(x_rim, f32),
                pltpu.VMEM(x_rim, f32),
                pltpu.VMEM(y_rim, f32),
                pltpu.VMEM(y_rim, f32),
                pltpu.VMEM((rows, column), f32),
                pltpu.VMEM((rows, column), f32),
                pltpu.SemaphoreType.DMA((11,)),
                pltpu.SemaphoreType.DMA((7,)),
                pltpu.SemaphoreType.DMA((7,)),
            ],
            compiler_params=pltpu.CompilerParams(collective_id=0, has_side_effects=True),
        )(
            conserved.reshape(full),
            troubled_list.reshape(1, -1),
            widths_x,
            widths_y,
            widths_z.reshape(1, -1),
            speed_x,
            speed_y,
            speed_z.reshape(1, -1),
        )
        advanced = pltpu.with_memory_space_constraint(advanced, pltpu.VMEM)
        hessian = pltpu.with_memory_space_constraint(hessian, pltpu.VMEM)
        advanced, hessian = pl.pallas_call(
            emit,
            out_shape=(
                jax.ShapeDtypeStruct(full, f32),
                jax.ShapeDtypeStruct((6, rows, column), f32),
            ),
            in_specs=[whole, whole],
            out_specs=(whole, whole),
            scratch_shapes=[pltpu.SemaphoreType.DMA((2,))],
        )(advanced, hessian)
        return advanced.reshape(conserved.shape), hessian.reshape(6, tile_x, tile_y, column)

    in_specs = (
        P(None, None, None, None, "gx", "gy", None),
        P(("gx", "gy")),
        P(),
        P(),
        P(),
        P(),
        P(),
        P(),
    )
    out_specs = (P(None, None, None, None, "gx", "gy", None), P(None, "gx", "gy", None))
    return jax.shard_map(local, mesh=mesh, in_specs=in_specs, out_specs=out_specs, check_vma=False)
```
